32 devices in a mesh: leaf: 4 (over y, core), row: 2 (over x), col: 4 (over z).
Axes of the slice: x: 2, y: 2, z: 4, core: 2. Of those that a mesh axis runs over, the one named last changes fastest.
Arguments:
- child_fronts: float32 [8192, 16384], P('col', ('leaf', 'row')), as said below
- arrow_entries: float32 [128, 16384], P(None, ('leaf', 'row')), as said below
- arrow_pattern: int32 [1, 127], replicated, may hold values 0 or 1
- child_maps: int32 [2, 63], replicated, may hold values from 0 to 125, as said below
Outputs:
- child_factored: float32 [8192, 16384], P('col', ('leaf', 'row'))
- root_front: float32 [16384, 16384], P('col', ('leaf', 'row'))
The draws below stay inside these ranges and needn't reach their ends.
Inputs may be any that keep to these rules, and one draw needn't show every extreme that they name: child_maps[k, i] is 2 i or 2 i + 1. `child_fronts`: each child front is symmetric and positive definite. The first 128 columns of arrow_entries form a symmetric positive definite matrix.
All inputs are finite; a program needn't handle non-finite values.
Results may differ from the reference program's by a relative error of at most 0.0001.
Values sent between devices are 32-bit elements; how exact they have to be, the bound alone decides.
A program may use at most 320 MiB of HBM per device.

```python
import math
import jax
import jax.numpy as jnp
from jax import lax

BLK = 128
NB0 = 128
SB = 1
F0 = 16384
F1 = 8192
UB = 63


def symmetric_part(key_values, key_diagonal, copies, order, bound):
    entries = jax.random.uniform(key_values, (copies, order, order), jnp.float32, -bound, bound)
    diagonal = jnp.exp(jax.random.uniform(key_diagonal, (copies, order), jnp.float32, math.log(2.5), math.log(5.0)))
    index = jnp.arange(order)
    above = index[None, :, None] < index[None, None, :]
    mirrored = jnp.where(above, entries, jnp.transpose(entries, (0, 2, 1)))
    on_diagonal = index[None, :, None] == index[None, None, :]
    return jnp.where(on_diagonal, diagonal[:, :, None], mirrored)


def draw_child_fronts(key, part):
    key_values, key_diagonal = jax.random.split(key)
    fronts = symmetric_part(key_values, key_diagonal, 2, F1, 1.5 / math.sqrt(F1))
    return jnp.concatenate([fronts[0], fronts[1]], axis=1)


def draw_arrow_entries(key, part):
    summed_width = SB * BLK
    key_values, key_diagonal, key_coupling = jax.random.split(key, 3)
    square = symmetric_part(key_values, key_diagonal, 1, summed_width, 1.5 / math.sqrt(summed_width))[0]
    bound = 1.5 / math.sqrt(F0)
    coupling = jax.random.uniform(key_coupling, (summed_width, F0 - summed_width), jnp.float32, -bound, bound)
    return jnp.concatenate([square, coupling], axis=1)


def draw_child_maps(key, part):
    key_parity, key_forced = jax.random.split(key)
    parity = jax.random.randint(key_parity, (2, UB), 0, 2, jnp.int32)
    forced_child = jax.random.randint(key_forced, (), 0, 2, jnp.int32)
    rows_of = jnp.arange(2, dtype=jnp.int32)[:, None]
    cols_of = jnp.arange(UB, dtype=jnp.int32)[None, :]
    parity = jnp.where(jnp.logical_and(rows_of == forced_child, cols_of == 0), 0, parity)
    parity = jnp.where(jnp.logical_and(rows_of != forced_child, cols_of == UB - 1), 1, parity)
    return 2 * cols_of + parity


def place_ends(values, own_key, least, high):
    index_at = [jax.random.randint(jax.random.fold_in(own_key, axis), (), 0, length) for axis, length in enumerate(values.shape)]
    widest = values.shape.index(max(values.shape))
    neighbour = index_at[:widest] + [(index_at[widest] + 1) % values.shape[widest]] + index_at[widest + 1:]
    return values.at[tuple(index_at)].set(least).at[tuple(neighbour)].set(high)


def setup_inputs(seed: int = 0) -> dict:
    key_of = jax.random.split(jax.random.key(seed), 5)
    child_fronts = draw_child_fronts(jax.random.fold_in(key_of[4], 71), 0)
    arrow_entries = draw_arrow_entries(jax.random.fold_in(key_of[4], 71), 0)
    arrow_pattern = place_ends((jax.random.randint(key_of[2], (SB, NB0 - SB), 0, 2) < 1).astype(jnp.int32), jax.random.fold_in(key_of[2], 1), 0, 1)
    child_maps = draw_child_maps(jax.random.fold_in(key_of[4], 71), 0)
    return dict(child_fronts=child_fronts, arrow_entries=arrow_entries, arrow_pattern=arrow_pattern, child_maps=child_maps)


def partial_factor(front):
    summed_width = SB * BLK
    front_order = front.shape[0]
    lower_factor = jnp.linalg.cholesky(front[:summed_width, :summed_width])
    solved = jax.scipy.linalg.solve_triangular(lower_factor, front[:summed_width, :], lower=True)
    keep_mask = jnp.arange(front_order)[None, :] >= jnp.arange(summed_width)[:, None]
    upper_rows = jnp.where(keep_mask, solved, 0.0)
    coupling = upper_rows[:, summed_width:]
    schur_part = front[summed_width:, summed_width:] - jnp.dot(coupling.T.astype(jnp.float32), coupling.astype(jnp.float32), preferred_element_type=jnp.float32, precision=lax.Precision.HIGHEST)
    result = jnp.zeros_like(front)
    result = result.at[:summed_width, :].set(upper_rows)
    return result.at[summed_width:, summed_width:].set(schur_part)

def reference(child_fronts, arrow_entries, arrow_pattern, child_maps):
    summed_width = SB * BLK
    offsets = jnp.arange(BLK, dtype=jnp.int32)
    assembled = jnp.zeros((F0, F0), jnp.float32)
    finished = []
    for child_index in range(2):
        factored = partial_factor(child_fronts[:, child_index * F1:(child_index + 1) * F1])
        finished.append(factored)
        positions = (child_maps[child_index][:, None] * BLK + offsets[None, :]).reshape(-1).astype(jnp.int32)
        assembled = assembled.at[positions[:, None], positions[None, :]].add(factored[summed_width:, summed_width:])
    full_pattern = jnp.concatenate([jnp.ones((SB, SB), jnp.int32), arrow_pattern], axis=1)
    keep_mask = jnp.repeat(jnp.repeat(full_pattern, BLK, axis=0), BLK, axis=1)
    masked = jnp.where(keep_mask > 0, arrow_entries, 0.0)
    parent = assembled.at[:summed_width, :].add(masked)
    return (jnp.concatenate(finished, axis=1), partial_factor(parent))
```

```python
import functools

import jax
import jax.numpy as jnp
from jax import lax
from jax.experimental import pallas as pl
from jax.experimental.pallas import tpu as pltpu
from jax.sharding import PartitionSpec as P

BLK = 128
UB = 63
PLANE = ("leaf", "row")
ALL = ("leaf", "row", "col")
HIGHEST = lax.Precision.HIGHEST


def split_two(x):
    high = lax.reduce_precision(x, 8, 7)
    return high.astype(jnp.bfloat16), (x - high).astype(jnp.bfloat16)


def left_terms(x):
    high, low = split_two(x)
    return jnp.concatenate([high, high, low, low], axis=-1)


def right_terms(x):
    high, low = split_two(x)
    return jnp.concatenate([high, low, high, low], axis=-2)


def factor(diagonal):
    lower = jnp.linalg.cholesky(diagonal)
    eye = jnp.broadcast_to(jnp.eye(BLK, dtype=jnp.float32), diagonal.shape)
    return jax.scipy.linalg.solve_triangular(lower, eye, lower=True)


def dot(a, b, contract):
    return lax.dot_general(
        a, b, (contract, ((), ())), precision=HIGHEST, preferred_element_type=jnp.float32
    )


def root_kernel(
    steps, half, scal, rpar, cpar, win_a, win_b, edge_a, edge_b, next_a, next_b, next_ea, next_eb,
    ur_a, ur_b, uc_a, uc_b, upr, upc, upf, out,
):
    i = pl.program_id(0)
    odd, first_col, first_row = scal[0], scal[1], scal[2]
    width = out.shape[1]
    chunk = min(512, width)
    for n in range(width // chunk):
        part = slice(n * chunk, (n + 1) * chunk)
        out[:, part] = -jnp.dot(upr[...], upc[:, part], preferred_element_type=jnp.float32)
    last = i == steps - 1
    slots = (
        (win_a, edge_a, next_a, next_ea, ur_a, uc_a),
        (win_b, edge_b, next_b, next_eb, ur_b, uc_b),
    )
    for e, (win, edge, nwin, nedge, ur, uc) in enumerate(slots):
        rows = pl.ds(pl.multiple_of(rpar[e * steps + i] * BLK, BLK), BLK)
        for j in range(half):
            product = jnp.dot(
                ur[...], uc[:, j * BLK : (j + 1) * BLK], preferred_element_type=jnp.float32
            )
            if j < half - 1:
                take = pl.ds(pl.multiple_of((j + odd) * BLK, BLK), BLK)
                entry = jnp.where(last, nwin[:, take], win[:, take])
            else:
                take = pl.ds(j * BLK, BLK)
                plain = jnp.where(last, nwin[:, take], win[:, take])
                entry = jnp.where(odd == 1, jnp.where(last, nedge[...], edge[...]), plain)
            cols = pl.ds(pl.multiple_of((2 * j + cpar[e * half + j]) * BLK, BLK), BLK)
            out[rows, cols] += entry - product

    @pl.when(first_row == 1)
    def _():
        out[:, :BLK] = jnp.zeros((2 * BLK, BLK), jnp.float32)

    @pl.when(jnp.logical_and(first_col == 1, i == 0))
    def _():
        out[:BLK, :] = upf[...]


def local(child, arrow, arrow_pattern, child_maps):
    H, W = child.shape
    c = lax.axis_index("col")
    s = lax.axis_index(PLANE)
    G = lax.axis_size(PLANE)
    NC = lax.axis_size("col")
    pf = G // 2
    k = s // pf
    q = s - k * pf
    rb, half = H // BLK, W // BLK // 2
    odd = s % 2
    HW = half * BLK
    PH = 2 * H

    to_a = [(p, 2 * (p % pf) + p // pf) for p in range(G)]
    to_b = [(p, 2 * (p % pf) + 1 - p // pf) for p in range(G)]
    edge_0 = [(p, 2 * p - 1) for p in range(1, pf)]
    edge_1 = [(pf + p, 2 * p - 1) for p in range(1, pf)]

    def route(x):
        left = lax.slice_in_dim(x, BLK, BLK + HW, axis=1)
        start_a = jnp.where(k == 0, BLK, HW)
        start_b = jnp.where(k == 0, HW, BLK)
        del left
        a = lax.ppermute(lax.dynamic_slice_in_dim(x, start_a, HW, 1), PLANE, to_a)
        b = lax.ppermute(lax.dynamic_slice_in_dim(x, start_b, HW, 1), PLANE, to_b)
        ea = lax.ppermute(x[:, :BLK], PLANE, edge_1)
        eb = lax.ppermute(x[:, :BLK], PLANE, edge_0)
        return a, b, ea, eb

    on_col = c == 0
    kids = jnp.arange(2)
    head = jnp.where(jnp.logical_and(on_col, q == 0), child[:BLK, :BLK], 0.0)
    diagonals = lax.psum(jnp.where((kids == k)[:, None, None], head[None], 0.0), ALL)
    raw_cols = lax.psum(jnp.where(on_col, child[:BLK, :], 0.0), "col")
    own_edge = jnp.where(q == 0, child[:, :BLK], 0.0)
    raw_rows = lax.psum(jnp.where((kids == k)[:, None, None], own_edge[None], 0.0), PLANE)
    back = [(p + 1, p) for p in range(NC - 1)]
    below = lax.ppermute(child[:BLK, :], "col", back)
    rows_below = lax.ppermute(raw_rows[:, :BLK], "col", back)

    bulk_a, bulk_b, bulk_ea, bulk_eb = route(child)

    inverses = factor(diagonals)
    own_inverse = jnp.where(k == 0, inverses[0], inverses[1])
    second_index = q * W + jnp.arange(W)
    upper = second_index[None, :] >= jnp.arange(BLK)[:, None]
    u_cols = jnp.where(upper, dot(own_inverse, raw_cols, ((1,), (0,))), 0.0)
    raw_ext = jnp.concatenate([raw_rows, rows_below], axis=1)
    u_rows = jnp.stack([dot(raw_ext[e], inverses[e], ((1,), (1,))) for e in range(2)])
    own_rows = jnp.where(k == 0, u_rows[0, :H], u_rows[1, :H])
    second_block = child[BLK : 2 * BLK, :] - dot(own_rows[BLK : 2 * BLK], u_cols, ((1,), (0,)))

    small = jnp.concatenate([u_cols, second_block, below], axis=0)
    small_a, small_b, small_ea, small_eb = route(small)

    def aligned(win, edge):
        shifted = jnp.concatenate([win, edge], axis=1)
        return jnp.where(odd == 1, shifted[:, BLK:], win)

    heads = [aligned(w[: 2 * BLK], e[: 2 * BLK]) for w, e in ((small_a, small_ea), (small_b, small_eb))]

    maps = jnp.concatenate([child_maps % 2, jnp.zeros((2, G * half - UB), jnp.int32)], axis=1)
    maps = jnp.where(odd == 1, maps[::-1], maps)
    row_par = lax.dynamic_slice_in_dim(maps, c * rb, rb, 1)
    col_par = lax.dynamic_slice_in_dim(maps, s * half, half, 1)

    full_pattern = jnp.concatenate([jnp.ones((1, 1), jnp.int32), arrow_pattern], axis=1)
    pattern_here = lax.dynamic_slice_in_dim(full_pattern, s * 2 * half, 2 * half, 1)
    keep = jnp.repeat(pattern_here, BLK, axis=1)
    pivot = jnp.where(keep > 0, arrow, 0.0)
    for e in range(2):
        given = heads[e][BLK:]
        pieces = []
        for j in range(half):
            block = given[:, j * BLK : (j + 1) * BLK]
            for a in range(2):
                here = jnp.logical_and(maps[e, 0] == 0, col_par[e, j] == a)
                pieces.append(jnp.where(here, block, 0.0))
        pivot = pivot + jnp.concatenate(pieces, axis=1)
    pivot = jnp.where(on_col, pivot, 0.0)
    root_diagonal = lax.psum(
        jnp.where(s == 0, pivot[:, :BLK], 0.0), ALL
    )
    pivot_cols = lax.psum(pivot, "col")
    sources = PH // W
    place = jnp.arange(sources) == s - sources * c
    pivot_rows = lax.psum(jnp.where(place[:, None, None], pivot_cols[None], 0.0), PLANE)
    root_inverse = factor(root_diagonal)
    root_index = s * W + jnp.arange(W)
    root_upper = root_index[None, :] >= jnp.arange(BLK)[:, None]
    up_cols = jnp.where(root_upper, dot(root_inverse, pivot_cols, ((1,), (0,))), 0.0)
    up_rows = jnp.concatenate(
        [dot(pivot_rows[e], root_inverse, ((0,), (1,))) for e in range(sources)], axis=0
    )

    first_index = c * H + jnp.arange(H)
    product = dot(own_rows, u_cols, ((1,), (0,)))
    trailing = jnp.logical_and(first_index[:, None] >= BLK, second_index[None, :] >= BLK)
    child_result = jnp.where(trailing, child - product, 0.0)
    child_result = child_result.at[:BLK].set(jnp.where(on_col, u_cols, child_result[:BLK]))

    slot_rows = jnp.where(odd == 1, u_rows[::-1], u_rows)[:, BLK:]
    scal = jnp.stack([odd, on_col.astype(jnp.int32), (s == 0).astype(jnp.int32)]).astype(jnp.int32)
    down = lambda i, *_: (jnp.minimum(i + 1, rb - 1), 0)
    fixed = lambda i, *_: (0, 0)
    step = lambda i, *_: (i, 0)
    in_specs = [
        pl.BlockSpec((BLK, HW), down),
        pl.BlockSpec((BLK, HW), down),
        pl.BlockSpec((BLK, BLK), down),
        pl.BlockSpec((BLK, BLK), down),
        pl.BlockSpec((BLK, HW), fixed),
        pl.BlockSpec((BLK, HW), fixed),
        pl.BlockSpec((BLK, BLK), fixed),
        pl.BlockSpec((BLK, BLK), fixed),
        pl.BlockSpec((BLK, 4 * BLK), step),
        pl.BlockSpec((BLK, 4 * BLK), step),
        pl.BlockSpec((4 * BLK, HW), fixed),
        pl.BlockSpec((4 * BLK, HW), fixed),
        pl.BlockSpec((2 * BLK, 4 * BLK), step),
        pl.BlockSpec((4 * BLK, W), fixed),
        pl.BlockSpec((BLK, W), fixed),
    ]
    root_result = pl.pallas_call(
        functools.partial(root_kernel, rb, half),
        out_shape=jax.ShapeDtypeStruct((PH, W), jnp.float32),
        grid_spec=pltpu.PrefetchScalarGridSpec(
            num_scalar_prefetch=3,
            grid=(rb,),
            in_specs=in_specs,
            out_specs=pl.BlockSpec((2 * BLK, W), step),
        ),
        compiler_params=pltpu.CompilerParams(vmem_limit_bytes=40 << 20),
        name="root_front",
    )(
        scal, row_par.reshape(-1), col_par.reshape(-1),
        bulk_a, bulk_b, bulk_ea, bulk_eb,
        small_a[2 * BLK :], small_b[2 * BLK :], small_ea[2 * BLK :], small_eb[2 * BLK :],
        left_terms(slot_rows[0]), left_terms(slot_rows[1]),
        right_terms(heads[0][:BLK]), right_terms(heads[1][:BLK]),
        left_terms(up_rows), right_terms(up_cols), up_cols,
    )
    return child_result, root_result


def solution(mesh):
    placed = (P("col", PLANE), P(None, PLANE), P(), P())
    return jax.shard_map(
        local,
        mesh=mesh,
        in_specs=placed,
        out_specs=(P("col", PLANE), P("col", PLANE)),
        check_vma=False,
    )
```

```python
import functools

import jax
import jax.numpy as jnp
from jax import lax
from jax.experimental import pallas as pl
from jax.experimental.pallas import tpu as pltpu
from jax.sharding import PartitionSpec as P

BLK = 128
UB = 63
PLANE = ("leaf", "row")
ALL = ("leaf", "row", "col")
HIGHEST = lax.Precision.HIGHEST


def split_two(x):
    high = lax.reduce_precision(x, 8, 7)
    return high.astype(jnp.bfloat16), (x - high).astype(jnp.bfloat16)


def left_terms(x):
    high, low = split_two(x)
    return jnp.concatenate([high, high, low, low], axis=-1)


def right_terms(x):
    high, low = split_two(x)
    return jnp.concatenate([high, low, high, low], axis=-2)


def factor(diagonal):
    lower = jnp.linalg.cholesky(diagonal)
    eye = jnp.broadcast_to(jnp.eye(BLK, dtype=jnp.float32), diagonal.shape)
    return jax.scipy.linalg.solve_triangular(lower, eye, lower=True)


def dot(a, b, contract):
    return lax.dot_general(
        a, b, (contract, ((), ())), precision=HIGHEST, preferred_element_type=jnp.float32
    )


def root_kernel(
    steps, half, scal, rpar, cpar, win_a, win_b, edge_a, edge_b, next_a, next_b, next_ea, next_eb,
    ur_a, ur_b, uc_a, uc_b, upr, upc, upf, out,
):
    i = pl.program_id(0)
    odd, first_col, first_row = scal[0], scal[1], scal[2]
    width = out.shape[1]
    chunk = min(512, width)
    for n in range(width // chunk):
        part = slice(n * chunk, (n + 1) * chunk)
        out[:, part] = -jnp.dot(upr[...], upc[:, part], preferred_element_type=jnp.float32)
    last = i == steps - 1
    slots = (
        (win_a, edge_a, next_a, next_ea, ur_a, uc_a),
        (win_b, edge_b, next_b, next_eb, ur_b, uc_b),
    )
    for e, (win, edge, nwin, nedge, ur, uc) in enumerate(slots):
        rows = pl.ds(pl.multiple_of(rpar[e * steps + i] * BLK, BLK), BLK)
        for j in range(half):
            product = jnp.dot(
                ur[...], uc[:, j * BLK : (j + 1) * BLK], preferred_element_type=jnp.float32
            )
            if j < half - 1:
                take = pl.ds(pl.multiple_of((j + odd) * BLK, BLK), BLK)
                entry = jnp.where(last, nwin[:, take], win[:, take])
            else:
                take = pl.ds(j * BLK, BLK)
                plain = jnp.where(last, nwin[:, take], win[:, take])
                entry = jnp.where(odd == 1, jnp.where(last, nedge[...], edge[...]), plain)
            cols = pl.ds(pl.multiple_of((2 * j + cpar[e * half + j]) * BLK, BLK), BLK)
            out[rows, cols] += entry - product

    @pl.when(first_row == 1)
    def _():
        out[:, :BLK] = jnp.zeros((2 * BLK, BLK), jnp.float32)

    @pl.when(jnp.logical_and(first_col == 1, i == 0))
    def _():
        out[:BLK, :] = upf[...]


def local(child, arrow, arrow_pattern, child_maps):
    H, W = child.shape
    c = lax.axis_index("col")
    s = lax.axis_index(PLANE)
    G = lax.axis_size(PLANE)
    NC = lax.axis_size("col")
    pf = G // 2
    k = s // pf
    q = s - k * pf
    rb, half = H // BLK, W // BLK // 2
    odd = s % 2
    HW = half * BLK
    PH = 2 * H

    to_a = [(p, 2 * (p % pf) + p // pf) for p in range(G)]
    to_b = [(p, 2 * (p % pf) + 1 - p // pf) for p in range(G)]
    edge_0 = [(p, 2 * p - 1) for p in range(1, pf)]
    edge_1 = [(pf + p, 2 * p - 1) for p in range(1, pf)]

    def route(x):
        start_a = jnp.where(k == 0, BLK, HW)
        start_b = jnp.where(k == 0, HW, BLK)
        a = lax.ppermute(lax.dynamic_slice_in_dim(x, start_a, HW, 1), PLANE, to_a)
        b = lax.ppermute(lax.dynamic_slice_in_dim(x, start_b, HW, 1), PLANE, to_b)
        ea = lax.ppermute(x[:, :BLK], PLANE, edge_1)
        eb = lax.ppermute(x[:, :BLK], PLANE, edge_0)
        return a, b, ea, eb

    on_col = c == 0
    kids = jnp.arange(2)
    head = jnp.where(jnp.logical_and(on_col, q == 0), child[:BLK, : 2 * BLK], 0.0)
    diagonals = lax.psum(jnp.where((kids == k)[:, None, None], head[None], 0.0), ALL)
    raw_cols = lax.psum(jnp.where(on_col, child[: 2 * BLK, :], 0.0), "col")
    own_edge = jnp.where(q == 0, child[:, :BLK], 0.0)
    raw_rows = lax.psum(jnp.where((kids == k)[:, None, None], own_edge[None], 0.0), PLANE)
    back = [(p + 1, p) for p in range(NC - 1)]
    below = lax.ppermute(child[:BLK, :], "col", back)
    rows_below = lax.ppermute(raw_rows[:, :BLK], "col", back)

    bulk = route(child)
    bulk, raw_cols, raw_rows, rows_below, below = lax.optimization_barrier(
        (bulk, raw_cols, raw_rows, rows_below, below)
    )
    bulk_a, bulk_b, bulk_ea, bulk_eb = bulk

    inverses = factor(diagonals[:, :, :BLK])
    own_inverse = jnp.where(k == 0, inverses[0], inverses[1])
    second_index = q * W + jnp.arange(W)
    upper = second_index[None, :] >= jnp.arange(BLK)[:, None]
    u_cols = jnp.where(upper, dot(own_inverse, raw_cols[:BLK], ((1,), (0,))), 0.0)
    raw_ext = jnp.concatenate([raw_rows, rows_below], axis=1)
    u_rows = jnp.stack([dot(raw_ext[e], inverses[e], ((1,), (1,))) for e in range(2)])
    own_rows = jnp.where(k == 0, u_rows[0, :H], u_rows[1, :H])
    own_second = jnp.where(k == 0, diagonals[0, :, BLK:], diagonals[1, :, BLK:])
    u_second = dot(own_inverse, own_second, ((1,), (0,)))
    second_block = raw_cols[BLK:] - dot(u_second, u_cols, ((0,), (0,)))

    small = jnp.concatenate([u_cols, second_block, below], axis=0)
    small_a, small_b, small_ea, small_eb = route(small)

    def aligned(win, edge):
        shifted = jnp.concatenate([win, edge], axis=1)
        return jnp.where(odd == 1, shifted[:, BLK:], win)

    heads = [aligned(w[: 2 * BLK], e[: 2 * BLK]) for w, e in ((small_a, small_ea), (small_b, small_eb))]

    maps = jnp.concatenate([child_maps % 2, jnp.zeros((2, G * half - UB), jnp.int32)], axis=1)
    maps = jnp.where(odd == 1, maps[::-1], maps)
    row_par = lax.dynamic_slice_in_dim(maps, c * rb, rb, 1)
    col_par = lax.dynamic_slice_in_dim(maps, s * half, half, 1)

    full_pattern = jnp.concatenate([jnp.ones((1, 1), jnp.int32), arrow_pattern], axis=1)
    pattern_here = lax.dynamic_slice_in_dim(full_pattern, s * 2 * half, 2 * half, 1)
    keep = jnp.repeat(pattern_here, BLK, axis=1)
    pivot = jnp.where(keep > 0, arrow, 0.0)
    for e in range(2):
        given = heads[e][BLK:]
        pieces = []
        for j in range(half):
            block = given[:, j * BLK : (j + 1) * BLK]
            for a in range(2):
                here = jnp.logical_and(maps[e, 0] == 0, col_par[e, j] == a)
                pieces.append(jnp.where(here, block, 0.0))
        pivot = pivot + jnp.concatenate(pieces, axis=1)
    root_diagonal = lax.psum(jnp.where(s == 0, pivot[:, :BLK], 0.0), PLANE)
    pivot_cols = pivot
    sources = PH // W
    place = jnp.arange(sources) == s - sources * c
    pivot_rows = lax.psum(jnp.where(place[:, None, None], pivot_cols[None], 0.0), PLANE)
    root_inverse = factor(root_diagonal)
    root_index = s * W + jnp.arange(W)
    root_upper = root_index[None, :] >= jnp.arange(BLK)[:, None]
    up_cols = jnp.where(root_upper, dot(root_inverse, pivot_cols, ((1,), (0,))), 0.0)
    up_rows = jnp.concatenate(
        [dot(pivot_rows[e], root_inverse, ((0,), (1,))) for e in range(sources)], axis=0
    )

    first_index = c * H + jnp.arange(H)
    product = dot(own_rows, u_cols, ((1,), (0,)))
    trailing = jnp.logical_and(first_index[:, None] >= BLK, second_index[None, :] >= BLK)
    child_result = jnp.where(trailing, child - product, 0.0)
    child_result = child_result.at[:BLK].set(jnp.where(on_col, u_cols, child_result[:BLK]))

    slot_rows = jnp.where(odd == 1, u_rows[::-1], u_rows)[:, BLK:]
    scal = jnp.stack([odd, on_col.astype(jnp.int32), (s == 0).astype(jnp.int32)]).astype(jnp.int32)
    down = lambda i, *_: (jnp.minimum(i + 1, rb - 1), 0)
    fixed = lambda i, *_: (0, 0)
    step = lambda i, *_: (i, 0)
    in_specs = [
        pl.BlockSpec((BLK, HW), down),
        pl.BlockSpec((BLK, HW), down),
        pl.BlockSpec((BLK, BLK), down),
        pl.BlockSpec((BLK, BLK), down),
        pl.BlockSpec((BLK, HW), fixed),
        pl.BlockSpec((BLK, HW), fixed),
        pl.BlockSpec((BLK, BLK), fixed),
        pl.BlockSpec((BLK, BLK), fixed),
        pl.BlockSpec((BLK, 4 * BLK), step),
        pl.BlockSpec((BLK, 4 * BLK), step),
        pl.BlockSpec((4 * BLK, HW), fixed),
        pl.BlockSpec((4 * BLK, HW), fixed),
        pl.BlockSpec((2 * BLK, 4 * BLK), step),
        pl.BlockSpec((4 * BLK, W), fixed),
        pl.BlockSpec((BLK, W), fixed),
    ]
    root_result = pl.pallas_call(
        functools.partial(root_kernel, rb, half),
        out_shape=jax.ShapeDtypeStruct((PH, W), jnp.float32),
        grid_spec=pltpu.PrefetchScalarGridSpec(
            num_scalar_prefetch=3,
            grid=(rb,),
            in_specs=in_specs,
            out_specs=pl.BlockSpec((2 * BLK, W), step),
        ),
        compiler_params=pltpu.CompilerParams(vmem_limit_bytes=40 << 20),
        name="root_front",
    )(
        scal, row_par.reshape(-1), col_par.reshape(-1),
        bulk_a, bulk_b, bulk_ea, bulk_eb,
        small_a[2 * BLK :], small_b[2 * BLK :], small_ea[2 * BLK :], small_eb[2 * BLK :],
        left_terms(slot_rows[0]), left_terms(slot_rows[1]),
        right_terms(heads[0][:BLK]), right_terms(heads[1][:BLK]),
        left_terms(up_rows), right_terms(up_cols), up_cols,
    )
    return child_result, root_result


def solution(mesh):
    placed = (P("col", PLANE), P(None, PLANE), P(), P())
    return jax.shard_map(
        local,
        mesh=mesh,
        in_specs=placed,
        out_specs=(P("col", PLANE), P("col", PLANE)),
        check_vma=False,
    )
```
